32 devices in a mesh: sector: 4 (over y, x), block: 8 (over z, core).
Axes of the slice: x: 2, y: 2, z: 4, core: 2. Of those that a mesh axis runs over, the one named last changes fastest.
Arguments:
- fields: float32 [5, 512, 64, 128], P(None, 'sector', 'block'), may hold values from -6 to 6
- local_inverse: float32 [5, 512, 128], P(None, 'sector'), may hold values from -1 to 1, as said below
- coupling: float32 [5, 64], replicated, may hold values from 0.45 to 0.65
- radial_rate: float32 [5, 64], replicated, may hold values from 0.2 to 0.8
- parcel_source: bfloat16 [5, 4, 64, 256], P(None, 'sector', 'block'), may hold values from -3 to 3
- parcel_cell: int32 [4, 64, 256], P('sector', 'block'), may hold values from 0 to 131071
- parcel_count: int32 [4, 64], P('sector', 'block'), may hold values from 0 to 256, as said below
Outputs:
- updated: float32 [5, 512, 64, 128], P(None, 'sector', 'block')
The draws below stay inside these ranges and needn't reach their ends.
Inputs may be any that keep to these rules, and one draw needn't show every extreme that they name: `parcel_count`: in every sector, one in eight of the owner blocks (at least one), chosen anew in every draw, receive a count of 256 from every sending block; every other count is at most 128. `local_inverse`: for every field, sector and radial row, coupling times the sum of the magnitudes of the first and last entries of the block's first row stays below 0.95, and likewise for its last row.
All inputs are finite; a program needn't handle non-finite values.
Results may differ from the reference program's by a relative error of at most 0.0003.
Values may be sent and summed in bfloat16 or wider, within the bound.
No kernel may reach another device: no remote copies, remote signals or barrier semaphores. Data moves between devices by JAX's collectives and lax.ppermute only.
A program may use at most 64 MiB of HBM per device.

```python
import math
import jax
import jax.numpy as jnp
from jax import lax

FIELDS = 5
NA = 128
RR = 8
AX = 128
CAP = 256
SECTORS = 4
OWNERS = 8
AZ = 512
NR = 64
CELLS = 131072


def draw_local_inverse(key, part):
    first_key, second_key, third_key = jax.random.split(key, 3)
    array_shape = (FIELDS, AZ, NA)
    spread = jax.random.uniform(first_key, array_shape, jnp.float32, -1.0, 1.0) * (0.5 / math.sqrt(NA))
    diagonal = jax.random.uniform(second_key, array_shape, jnp.float32, 0.5, 1.0)
    border = jax.random.uniform(third_key, array_shape, jnp.float32, 0.3, 0.7)
    row_index = (jnp.arange(AZ) % NA)[None, :, None]
    col_index = jnp.arange(NA)[None, None, :]
    matrix = jnp.where(row_index == col_index, diagonal, spread)
    return jnp.where((col_index == 0) | (col_index == NA - 1), border, matrix)


def draw_parcel_count(key, part):
    order_keys = jax.random.split(jax.random.fold_in(key, 11), SECTORS)
    orders = jax.vmap(lambda one_key: jax.random.permutation(one_key, OWNERS))(order_keys)
    heavy_count = max(1, OWNERS // 8)
    heavy = jnp.any(orders[:, :heavy_count, None] == jnp.arange(OWNERS)[None, None, :], axis=1)
    light = jax.random.randint(jax.random.fold_in(key, 12), (SECTORS, OWNERS, OWNERS), 0, CAP // 2 + 1)
    counts = jnp.where(heavy[:, None, :], CAP, light)
    return counts.reshape(SECTORS, OWNERS * OWNERS).astype(jnp.int32)


def with_ends(values, own_key, smallest, high):
    longest = values.shape.index(max(values.shape))
    spots = []
    for shift in (0, 1):
        where = [jax.random.randint(jax.random.fold_in(own_key, axis), (), 0, length) for axis, length in enumerate(values.shape)]
        where[longest] = (where[longest] + shift) % values.shape[longest]
        spots.append(tuple(where))
    return values.at[spots[0]].set(smallest).at[spots[1]].set(high)


def block_scale(own_key, shape, cuts, smallest, top_value):
    loudness = 1.0
    for axis_at, blocks in cuts:
        steps = jax.random.uniform(jax.random.fold_in(jax.random.fold_in(own_key, 6), axis_at), (blocks,), jnp.float32, smallest / len(cuts), top_value / len(cuts))
        loudness = loudness * jnp.repeat(jnp.exp(steps), shape[axis_at] // blocks).reshape((-1,) + (1,) * (len(shape) - 1 - axis_at))
    return loudness


def scatter_about(stream_key, extent, width, bound, cuts=(), kind=jnp.bfloat16):
    values = jax.random.normal(stream_key, extent, jnp.float32) * width
    if len(cuts) > 0:
        values = block_scale(stream_key, extent, cuts, -0.22, 0.18) * values
    return jnp.clip(values, min=-bound, max=bound).astype(kind)


def setup_inputs(seed: int = 0) -> dict:
    keys = jax.random.split(jax.random.key(seed), 8)
    fields = scatter_about(keys[0], (FIELDS, AZ, NR, AX), 1.0, 6.0, ((1, 4), (2, 8)), jnp.float32)
    local_inverse = draw_local_inverse(jax.random.fold_in(keys[7], 71), 0)
    coupling = jnp.clip(jax.random.uniform(keys[2], (FIELDS, NR), jnp.float32, 0.45, 0.65), 0.45, 0.65)
    radial_rate = jnp.clip(jnp.exp(jax.random.uniform(keys[3], (FIELDS, NR), jnp.float32, math.log(0.2), math.log(0.8))), 0.2, 0.8)
    parcel_source = scatter_about(keys[4], (FIELDS, SECTORS, OWNERS * OWNERS, CAP), 0.5, 3.0, ((1, 4), (2, 8)))
    parcel_cell = with_ends(jax.random.randint(keys[5], (SECTORS, OWNERS * OWNERS, CAP), 0, CELLS), jax.random.fold_in(keys[5], 1), 0, CELLS - 1).astype(jnp.int32)
    parcel_count = draw_parcel_count(jax.random.fold_in(keys[7], 71), 0)
    return {"fields": fields, "local_inverse": local_inverse, "coupling": coupling, "radial_rate": radial_rate, "parcel_source": parcel_source, "parcel_cell": parcel_cell, "parcel_count": parcel_count}


precise = lax.Precision.HIGHEST

def radial_term(field, rates):
    row_count = field.shape[2]
    padded = jnp.pad(field, ((0, 0), (0, 0), (2, 2), (0, 0)))
    close_sum = padded[:, :, 1:row_count + 1] + padded[:, :, 3:row_count + 3]
    outer_sum = padded[:, :, 0:row_count] + padded[:, :, 4:row_count + 4]
    return rates[:, None, :, None] * (16.0 * close_sum - outer_sum - 30.0 * field) / 12.0

def cyclic_solve(right_side, local_inverse, coupling):
    field_count, azimuth_len, radial_len, axial_len = right_side.shape
    sector_count = azimuth_len // NA
    blocks = local_inverse.reshape(field_count, sector_count, NA, NA)
    pieces = right_side.reshape(field_count, sector_count, NA, radial_len, axial_len)
    local_part = jnp.einsum('fsab,fsbrx->fsarx', blocks, pieces, precision=precise)
    first_col = blocks[:, :, :, 0]
    last_col = blocks[:, :, :, NA - 1]
    sector_ids = jnp.arange(sector_count)
    prev_shift = (sector_ids[None, :] == (sector_ids[:, None] - 1) % sector_count).astype(jnp.float32)
    next_shift = (sector_ids[None, :] == (sector_ids[:, None] + 1) % sector_count).astype(jnp.float32)
    k_ll = prev_shift[None] * blocks[:, None, :, NA - 1, 0]
    k_lr = prev_shift[None] * blocks[:, None, :, NA - 1, NA - 1]
    k_rl = next_shift[None] * blocks[:, None, :, 0, 0]
    k_rr = next_shift[None] * blocks[:, None, :, 0, NA - 1]
    kernel = jnp.concatenate([jnp.concatenate([k_ll, k_lr], 2), jnp.concatenate([k_rl, k_rr], 2)], 1)
    unit_matrix = jnp.eye(2 * sector_count, dtype=jnp.float32)
    system = unit_matrix[None, None] - coupling[:, :, None, None] * kernel[:, None]
    left_known = jnp.roll(local_part[:, :, NA - 1], 1, axis=1)
    right_known = jnp.roll(local_part[:, :, 0], -1, axis=1)
    known_side = jnp.concatenate([left_known, right_known], 1).transpose(0, 2, 1, 3)
    solved = jnp.linalg.solve(system, known_side)
    left_ends = solved[:, :, :sector_count].transpose(0, 2, 1, 3)
    right_ends = solved[:, :, sector_count:].transpose(0, 2, 1, 3)
    weights = coupling[:, None, None, :, None]
    result = local_part + weights * (left_ends[:, :, None] * first_col[:, :, :, None, None] + right_ends[:, :, None] * last_col[:, :, :, None, None])
    return result.reshape(field_count, azimuth_len, radial_len, axial_len)

def deposit(parcel_source, parcel_cell, parcel_count):
    field_count, sector_count, pair_count, slot_count = parcel_source.shape
    live_mask = jnp.arange(slot_count, dtype=jnp.int32)[None, None, :] < parcel_count[:, :, None]
    values = jnp.where(live_mask[None], parcel_source.astype(jnp.float32), 0.0)
    owner_ids = jnp.arange(pair_count, dtype=jnp.int32) % OWNERS
    target = (jnp.arange(sector_count, dtype=jnp.int32)[:, None, None] * OWNERS + owner_ids[None, :, None]) * CELLS + parcel_cell
    contrib = values.reshape(field_count, -1).T
    summed = jax.ops.segment_sum(contrib, target.reshape(-1), num_segments=sector_count * OWNERS * CELLS)
    deposited = summed.reshape(sector_count, OWNERS, NA, RR, AX, field_count)
    return deposited.transpose(5, 0, 2, 1, 3, 4).reshape(field_count, sector_count * NA, OWNERS * RR, AX)

def reference(fields, local_inverse, coupling, radial_rate, parcel_source, parcel_cell, parcel_count):
    source = deposit(parcel_source, parcel_cell, parcel_count)
    rhs_first = fields + radial_term(fields, radial_rate) + source
    middle = cyclic_solve(rhs_first, local_inverse, coupling)
    rhs_second = middle + radial_term(middle, radial_rate) + source
    return cyclic_solve(rhs_second, local_inverse, coupling)
```

```python
import functools

import jax
import jax.numpy as jnp
from jax import lax
from jax.experimental import pallas as pl
from jax.experimental.pallas import tpu as pltpu
from jax.sharding import PartitionSpec as P

F32 = jnp.float32
BF16 = jnp.bfloat16
HALO = 2
WIDE = 2 * HALO

VMEM = pl.BlockSpec(memory_space=pltpu.VMEM)
SMEM = pl.BlockSpec(memory_space=pltpu.SMEM)


def call(kernel, out_shape, in_specs, scratch=(), flops=1_000_000, moved=1_000_000, name=None):
    single = not isinstance(out_shape, (tuple, list))
    return pl.pallas_call(
        kernel,
        out_shape=out_shape,
        in_specs=list(in_specs),
        out_specs=VMEM if single else [VMEM] * len(out_shape),
        scratch_shapes=list(scratch),
        cost_estimate=pl.CostEstimate(flops=flops, bytes_accessed=moved, transcendentals=0),
        name=name,
    )


def split(value):
    high = value.astype(BF16)
    low = (value - high.astype(F32)).astype(BF16)
    return high, low


def prepare_kernel(inv_ref, high_ref, low_ref, cols_ref, rows_ref, corner_ref):
    count, size = inv_ref.shape[:2]

    def one(f, carry):
        inverse = inv_ref[f]
        square = jnp.dot(
            inverse, inverse, preferred_element_type=F32, precision=lax.Precision.HIGHEST
        )
        both = jnp.concatenate([square, inverse], 1)
        high, low = split(both)
        high_ref[f] = high
        low_ref[f] = low
        for k, matrix in enumerate((square, inverse)):
            flipped = matrix.T
            for e, at in enumerate((0, size - 1)):
                column = jnp.broadcast_to(matrix[:, at : at + 1], (size, size))
                row = jnp.broadcast_to(flipped[:, at : at + 1], (size, size))
                cols_ref[f, 2 * k + e] = column
                rows_ref[f, 2 * k + e] = row
                for d, place in enumerate((0, size - 1)):
                    slot = 4 * k + 2 * d + e
                    corner_ref[f, slot : slot + 1] = column[place : place + 1]
        return carry

    lax.fori_loop(0, count, one, 0)


def deposit_kernel(sizes, got_ref, src_ref, hot_ref, spread_ref):
    fields, azimuth, rows, axial, senders, cap = sizes
    comps = fields + 3
    half = cap // 2
    cell_ids = lax.broadcasted_iota(jnp.int32, (azimuth, half), 0).astype(F32).astype(BF16)
    axial_ids = lax.broadcasted_iota(jnp.int32, (axial, half), 0).astype(F32).astype(BF16)
    zero = jnp.zeros((), BF16)
    one = jnp.ones((), BF16)

    def add(which, part, targets, first):
        lanes = slice(part * half, (part + 1) * half)
        for s in range(senders):
            block = got_ref[s, which * comps : (which + 1) * comps, lanes].astype(F32)
            cell = block[fields : fields + 1]
            row = block[fields + 1 : fields + 2]
            place = block[fields + 2 : fields + 3].astype(BF16)
            at = slice(s * half, (s + 1) * half)
            for m, (r, unused) in enumerate(targets):
                wanted = jnp.where(row == float(r), cell, -1.0).astype(BF16)
                hot = jnp.where(cell_ids == wanted, one, zero)
                hot_ref[m * azimuth : (m + 1) * azimuth, at] = hot
            here = axial_ids == place
            for f in range(fields):
                value = block[f : f + 1].astype(BF16)
                spread_ref[f * axial : (f + 1) * axial, at] = jnp.where(
                    here, jnp.broadcast_to(value, (axial, half)), zero
                )
        total = lax.dot_general(
            hot_ref[: len(targets) * azimuth],
            spread_ref[...],
            (((1,), (1,)), ((), ())),
            preferred_element_type=F32,
        )
        for m, (unused, out_row) in enumerate(targets):
            for f in range(fields):
                piece = total[m * azimuth : (m + 1) * azimuth, f * axial : (f + 1) * axial]
                span = slice(out_row * axial, (out_row + 1) * axial)
                if first:
                    src_ref[f, :, span] = piece
                else:
                    src_ref[f, :, span] += piece

    plans = (
        (1, [(r, r + HALO) for r in range(rows)]),
        (0, [(rows - HALO + k, k) for k in range(HALO)]),
        (2, [(k, rows + HALO + k) for k in range(HALO)]),
    )
    for which, targets in plans:
        add(which, 0, targets, True)
        late = got_ref[:, which * comps : which * comps + fields, half:].astype(F32)
        busy = jnp.max(jnp.abs(late)) > 0.0

        @pl.when(busy)
        def _():
            add(which, 1, targets, False)


def stencil_kernel(sizes, coef_ref, low_ref, own_ref, high_ref, src_ref, rows_ref, z_ref, ends_ref):
    fields, azimuth, rows, axial = sizes
    reach = rows + 2 * HALO
    chunk = 8

    def one(f, carry):
        coefs = [[coef_ref[c, f, i] for i in range(reach)] for c in range(3)]

        def step(n, sums):
            at = pl.ds(pl.multiple_of(n * chunk, chunk), chunk)
            weights = [rows_ref[f, k, at, :] for k in range(4)]

            def load(i):
                if i < WIDE:
                    return low_ref[f, at, i * axial : (i + 1) * axial]
                if i < WIDE + rows:
                    return own_ref[f, at, (i - WIDE) * axial : (i - WIDE + 1) * axial]
                j = i - WIDE - rows
                return high_ref[f, at, j * axial : (j + 1) * axial]

            def stencil(values, i, row):
                near = values[i - 1] + values[i + 1]
                far = values[i - 2] + values[i + 2]
                return coefs[0][row] * values[i] + coefs[1][row] * near + coefs[2][row] * far

            window = [load(i) for i in range(rows + 2 * WIDE)]
            source = [src_ref[f, at, i * axial : (i + 1) * axial] for i in range(reach)]
            rhs = [stencil(window, i + HALO, i) + source[i] for i in range(reach)]
            z = [stencil(rhs, i + HALO, i + HALO) for i in range(rows)]
            for i in range(rows):
                z_ref[f, at, i * axial : (i + 1) * axial] = z[i]
            fresh = []
            for e in range(2):
                fresh += [weights[2 + e] * rhs[i] for i in range(reach)]
            for e in range(2):
                fresh += [
                    weights[e] * z[i] + weights[2 + e] * source[i + HALO] for i in range(rows)
                ]
            return tuple(a + b for a, b in zip(sums, fresh))

        start = tuple(jnp.zeros((chunk, axial), F32) for k in range(2 * reach + 2 * rows))
        sums = lax.fori_loop(0, azimuth // chunk, step, start)
        lines = [jnp.sum(a, axis=0, keepdims=True) for a in sums]
        for e in range(2):
            for i in range(reach):
                ends_ref[f, e * reach + i : e * reach + i + 1] = lines[e * reach + i]
            for i in range(rows):
                at = 2 * reach + e * rows + i
                ends_ref[f, at : at + 1] = lines[at]
        return carry

    lax.fori_loop(0, fields, one, 0)


def product_kernel(sizes, high_ref, low_ref, z_ref, src_ref, out_ref):
    fields, azimuth, rows, axial = sizes

    def one(f, carry):
        z_high, z_low = split(z_ref[f])
        s_high, s_low = split(src_ref[f, :, HALO * axial : (HALO + rows) * axial])
        top = jnp.concatenate([z_high, s_high], 0)
        rest = jnp.concatenate([z_low, s_low], 0)
        a_high = high_ref[f]
        total = jnp.dot(a_high, rest, preferred_element_type=F32)
        total += jnp.dot(low_ref[f], top, preferred_element_type=F32)
        total += jnp.dot(a_high, top, preferred_element_type=F32)
        out_ref[f] = total
        return carry

    lax.fori_loop(0, fields, one, 0)


def ring_coefs(corners):
    a00, a0n, an0, ann = corners[0]
    fp, fq, lp, lq = a00, a0n, an0, ann
    steps = []
    for b00, b0n, bn0, bnn in corners[1:]:
        r = 1.0 / (1.0 - lq * b00)
        ep, eq = r * lp, r * lq * b0n
        qp, qq = b00 * ep, b00 * eq + b0n
        steps.append((r, lq, ep, eq, fq))
        fp, fq = fp + fq * qp, fq * qq
        lp, lq = bn0 * ep, bn0 * eq + bnn
    det = 1.0 / ((1.0 - lp) * (1.0 - fq) - lq * fp)
    return steps, (fp, fq, lp, lq, det)


def ring_solve(corners, coefs, heads, tails):
    steps, (fp, fq, lp, lq, det) = coefs
    first, last = heads[0], tails[0]
    kept = []
    for k, (r, lq_k, ep, eq, fq_k) in enumerate(steps):
        b00, b0n, bn0, bnn = corners[k + 1]
        e = r * (last + lq_k * heads[k + 1])
        first = first + fq_k * (heads[k + 1] + b00 * e)
        last = tails[k + 1] + bn0 * e
        kept.append((e, ep, eq))
    p0 = det * ((1.0 - fq) * last + lq * first)
    q = det * ((1.0 - lp) * first + fp * last)
    count = len(corners)
    ps, qs = [None] * count, [None] * count
    ps[0], qs[count - 1] = p0, q
    for k in range(count - 2, -1, -1):
        e, ep, eq = kept[k]
        b00, b0n, bn0, bnn = corners[k + 1]
        ps[k + 1] = e + ep * p0 + eq * qs[k + 1]
        qs[k] = heads[k + 1] + b00 * ps[k + 1] + b0n * qs[k + 1]
    return ps, qs


def finish_kernel(sizes, tab_ref, part_ref, cols_ref, *refs):
    fields, azimuth, rows, axial, sectors = sizes
    ends = refs[:sectors]
    out_ref, line_ref = refs[sectors], refs[sectors + 1]
    reach = rows + 2 * HALO
    base = 2 * reach + 2 * rows

    def one(f, carry):
        weight = tab_ref[0, f]
        coefs = [tab_ref[1 + c, f, HALO : HALO + rows] for c in range(3)]
        raw = []
        for s in range(sectors):
            raw.append([ends[s][f, base + k : base + k + 1] for k in range(8)])
        corners = [tuple(weight * raw[s][4 + k] for k in range(4)) for s in range(sectors)]
        setup = ring_coefs(corners)
        heads = [ends[s][f, 0:reach] for s in range(sectors)]
        tails = [ends[s][f, reach : 2 * reach] for s in range(sectors)]
        ps, qs = ring_solve(corners, setup, heads, tails)

        def stencil(value):
            value = weight * value
            near = value[1 : rows + 1] + value[3 : rows + 3]
            far = value[0:rows] + value[4 : rows + 4]
            return coefs[0] * value[HALO : HALO + rows] + coefs[1] * near + coefs[2] * far

        ps = [stencil(v) for v in ps]
        qs = [stencil(v) for v in qs]
        own = slice(HALO, HALO + rows)
        cut = lambda v: v[own]
        near_corners = [tuple(cut(c) for c in corners[s]) for s in range(sectors)]
        steps, close = setup
        near_setup = ([tuple(cut(c) for c in step) for step in steps], tuple(cut(c) for c in close))
        heads, tails = [], []
        for s in range(sectors):
            s00, s0n, sn0, snn = raw[s][:4]
            at = 2 * reach
            heads.append(ends[s][f, at : at + rows] + s00 * ps[s] + s0n * qs[s])
            tails.append(ends[s][f, at + rows : at + 2 * rows] + sn0 * ps[s] + snn * qs[s])
        ps2, qs2 = ring_solve(near_corners, near_setup, heads, tails)
        line_ref[0] = ps[0]
        line_ref[1] = qs[0]
        line_ref[2] = weight[own] * ps2[0]
        line_ref[3] = weight[own] * qs2[0]
        for r in range(rows):
            span = slice(r * axial, (r + 1) * axial)
            total = part_ref[f, :, span]
            for k in range(4):
                total += cols_ref[f, k] * line_ref[k, r : r + 1]
            out_ref[f, :, span] = total
        return carry

    lax.fori_loop(0, fields, one, 0)


def shards(fields, local_inverse, coupling, radial_rate, parcel_source, parcel_cell, parcel_count):
    count, azimuth, rows, axial = fields.shape
    sectors = lax.axis_size("sector")
    blocks = lax.axis_size("block")
    block_index = lax.axis_index("block")
    cap = parcel_source.shape[3]
    comps = count + 3
    reach = rows + 2 * HALO

    live = jnp.arange(cap, dtype=jnp.int32)[None, :] < parcel_count[0][:, None]
    values = jnp.where(live[None], parcel_source[:, 0], jnp.zeros((), BF16))
    cell = parcel_cell[0]
    coords = jnp.stack([cell // (rows * axial), cell // axial % rows, cell % axial])
    lists = jnp.concatenate([values, coords.astype(BF16)], 0).transpose(1, 0, 2)
    padded = jnp.pad(lists, ((1, 1), (0, 0), (0, 0)))
    outgoing = jnp.concatenate([padded[:-2], padded[1:-1], padded[2:]], 1)
    got = lax.all_to_all(outgoing, "block", split_axis=0, concat_axis=0, tiled=True)

    own = fields.reshape(count, azimuth, rows * axial)
    forward = [(i, i + 1) for i in range(blocks - 1)]
    backward = [(i + 1, i) for i in range(blocks - 1)]
    low = lax.ppermute(own[:, :, (rows - WIDE) * axial :], "block", forward)
    high = lax.ppermute(own[:, :, : WIDE * axial], "block", backward)

    table = jnp.stack(
        [coupling, 1.0 - 2.5 * radial_rate, radial_rate * (16.0 / 12.0), radial_rate * (-1.0 / 12.0)]
    )
    table = jnp.pad(table, ((0, 0), (0, 0), (HALO, HALO)))
    table = lax.dynamic_slice_in_dim(table, block_index * rows, reach, 2)
    wide_table = jnp.broadcast_to(table[..., None], table.shape + (axial,))

    shape = jax.ShapeDtypeStruct
    high_inv, low_inv, cols, lines, corner = call(
        prepare_kernel,
        [
            shape((count, azimuth, 2 * azimuth), BF16),
            shape((count, azimuth, 2 * azimuth), BF16),
            shape((count, 4, azimuth, axial), F32),
            shape((count, 4, azimuth, axial), F32),
            shape((count, 8, axial), F32),
        ],
        [VMEM],
        name="prepare",
    )(local_inverse)

    source = call(
        functools.partial(deposit_kernel, (count, azimuth, rows, axial, blocks, cap)),
        shape((count, azimuth, reach * axial), F32),
        [VMEM],
        [
            pltpu.VMEM((rows * azimuth, blocks * (cap // 2)), BF16),
            pltpu.VMEM((count * axial, blocks * (cap // 2)), BF16),
        ],
        flops=5_000_000_000,
        moved=8_000_000,
        name="deposit",
    )(got)

    sizes = (count, azimuth, rows, axial)
    z, ends = call(
        functools.partial(stencil_kernel, sizes),
        [
            shape((count, azimuth, rows * axial), F32),
            shape((count, 2 * reach + 2 * rows, axial), F32),
        ],
        [SMEM] + [VMEM] * 5,
        moved=12_000_000,
        name="stencil",
    )(table[1:], low, own, high, source, lines)

    payload = jnp.concatenate([ends, corner], 1)
    others = [
        lax.ppermute(payload, "sector", [((i + k) % sectors, i) for i in range(sectors)])
        for k in range(1, sectors)
    ]
    part = call(
        functools.partial(product_kernel, sizes),
        shape((count, azimuth, rows * axial), F32),
        [VMEM] * 4,
        flops=1_000_000_000,
        moved=12_000_000,
        name="product",
    )(high_inv, low_inv, z, source)

    out = call(
        functools.partial(finish_kernel, sizes + (sectors,)),
        shape((count, azimuth, rows * axial), F32),
        [VMEM] * (3 + sectors),
        [pltpu.VMEM((4, rows, axial), F32)],
        moved=8_000_000,
        name="finish",
    )(wide_table, part, cols, payload, *others)
    return out.reshape(fields.shape)


def solution(mesh):
    in_specs = (
        P(None, "sector", "block", None),
        P(None, "sector", None),
        P(),
        P(),
        P(None, "sector", "block", None),
        P("sector", "block", None),
        P("sector", "block"),
    )
    out_specs = P(None, "sector", "block", None)
    return jax.shard_map(shards, mesh=mesh, in_specs=in_specs, out_specs=out_specs, check_vma=False)
```
